32 devices in a mesh: groups: 2 (over x), gx: 16 (over z, y, core).
Axes of the slice: x: 2, y: 2, z: 4, core: 2. Of those that a mesh axis runs over, the one named last changes fastest.
Arguments:
- snapshots: bfloat16 [256, 4, 512, 128], P('gx', None, 'groups'), parts along dimension 2, may hold values from -20 to 20
- cell_weights: float32 [512, 128], P(('groups', 'gx')), parts along dimension 0, may hold values from 0.5 to 4.5
- diffusivity: float32 [4, 512, 128], P(None, ('groups', 'gx')), parts along dimension 1, may hold values from 0.2 to 2
Outputs:
- diffused_modes: bfloat16 [256, 4, 512, 128], P(None, None, ('groups', 'gx')), parts along dimension 2
- reduced_operator: float32 [512, 256], P('groups'), parts along dimension 0
The draws below stay inside these ranges and needn't reach their ends.
There are 2 independent parts, one for each index of `groups`. The reference program is written for one: setup_inputs(seed, part) draws one part's arguments, and reference() takes and returns one part's arrays. A program takes and returns all parts, laid end to end along the dimension named above; each array names one. Nothing has to cross between parts.
All inputs are finite; a program needn't handle non-finite values.
Results may differ from the reference program's by a relative error of at most 0.0005.
Values may be sent and summed in bfloat16 or wider, within the bound.
A program may use at most 128 MiB of HBM per device.

```python
import math
import jax
import jax.numpy as jnp
from jax import lax

S = 256
V = 4
PY = 128
NX = 256


def draw_snapshots(key, part):
    keys = jax.random.split(key, 4)
    amplitude = jnp.exp(jax.random.uniform(keys[0], (S, 1, 1, 1), minval=0.0, maxval=math.log(3.0)))
    noise = jax.random.truncated_normal(keys[1], -4.0, 4.0, (S, V, NX, PY))
    coeffs = jax.random.uniform(keys[2], (4, S, 1, 1, 1), minval=-0.6, maxval=0.6)
    pattern = jax.random.uniform(keys[3], (4, 1, V, NX, PY), minval=-1.0, maxval=1.0)
    shared = coeffs[0] * pattern[0] + coeffs[1] * pattern[1] + coeffs[2] * pattern[2] + coeffs[3] * pattern[3]
    return (amplitude * (noise + shared)).astype(jnp.bfloat16)


def draw_cell_weights(key, part):
    ramp = 1.0 + 2.0 * jnp.arange(NX, dtype=jnp.float32)[:, None] / (NX - 1)
    factor = jax.random.uniform(key, (NX, PY), minval=0.5, maxval=1.5)
    return ramp * factor


def shard_levels(rng, extent, shards, smallest, largest):
    def one(axis_at, parts):
        heights = jax.random.uniform(jax.random.fold_in(jax.random.fold_in(rng, 6), axis_at), (parts,), jnp.float32, smallest / len(shards), largest / len(shards))
        return jnp.repeat(jnp.exp(heights), extent[axis_at] // parts).reshape((-1,) + (1,) * (len(extent) - axis_at - 1))

    level = one(*shards[0])
    for cut in shards[1:]:
        level = level * one(*cut)
    return level


def setup_inputs(seed: int = 0, part: int = 0) -> dict:
    arg_keys = jax.random.split(jax.random.key(seed), 4)
    own_keys = jax.random.split(jax.random.fold_in(arg_keys[3], part), 4)
    snapshots = draw_snapshots(jax.random.fold_in(jax.random.fold_in(arg_keys[3], part), 71), part)
    cell_weights = draw_cell_weights(jax.random.fold_in(jax.random.fold_in(arg_keys[3], part), 71), part)
    diffusivity = jnp.clip(jnp.exp(math.log(2.0) - 2.3025851 * jax.random.uniform(own_keys[2], (V, NX, PY), jnp.float32) ** shard_levels(own_keys[2], (V, NX, PY), ((1, 16),), -0.2, 0.2)), 0.2, 2.0)
    return {"snapshots": snapshots, "cell_weights": cell_weights, "diffusivity": diffusivity}


def stencil_apply(padded_x, diffusivity):
    field = padded_x[:, :, 2:-2]
    along_x = (-padded_x[:, :, :-4] + 16.0 * padded_x[:, :, 1:-3] - 30.0 * field + 16.0 * padded_x[:, :, 3:-1] - padded_x[:, :, 4:]) / 12.0
    padded_y = jnp.pad(field, ((0, 0), (0, 0), (0, 0), (2, 2)))
    along_y = (-padded_y[..., :-4] + 16.0 * padded_y[..., 1:-3] - 30.0 * field + 16.0 * padded_y[..., 3:-1] - padded_y[..., 4:]) / 12.0
    return diffusivity * (along_x + along_y)

def reference(snapshots, cell_weights, diffusivity):
    hi = lax.Precision.HIGHEST
    cell_count = snapshots.shape[1] * snapshots.shape[2] * snapshots.shape[3]
    snap_float = snapshots.astype(jnp.float32)
    gram_total = jnp.einsum('svxy,tvxy->st', snap_float, snap_float * cell_weights, precision=hi) / cell_count
    lower_factor = jnp.linalg.cholesky(gram_total)
    identity = jnp.eye(gram_total.shape[0], dtype=jnp.float32)
    rotation = jax.scipy.linalg.solve_triangular(lower_factor, identity, lower=True)
    mode_field = jnp.einsum('st,tvxy->svxy', rotation, snap_float, precision=hi)
    padded_x = jnp.pad(mode_field, ((0, 0), (0, 0), (2, 2), (0, 0)))
    diffused = stencil_apply(padded_x, diffusivity)
    reduced = jnp.einsum('svxy,tvxy->st', mode_field * cell_weights, diffused, precision=hi) / cell_count
    return (diffused.astype(jnp.bfloat16), reduced)
```

```python
import functools

import jax
import jax.numpy as jnp
from jax import lax
from jax.experimental import pallas as pl
from jax.experimental.pallas import tpu as pltpu
from jax.sharding import PartitionSpec as P

MESH = pl.DeviceIdType.MESH
HIGHEST = lax.Precision.HIGHEST
NT = (((1,), (1,)), ((), ()))
TN = (((0,), (0,)), ((), ()))
PACK = 16
PIVOTS = 32
PANEL = 8
PAIR = 2
GATHER_VMEM = 54 * 2**20
MODES_VMEM = 40 * 2**20


def iota(shape, dim):
    return lax.broadcasted_iota(jnp.int32, shape, dim)


def swap_matrix(outer, inner):
    size = outer * inner
    row, col = iota((size, size), 0), iota((size, size), 1)
    source = lax.rem(row, inner) * outer + lax.div(row, inner)
    return jnp.where(col == source, 1.0, 0.0).astype(jnp.bfloat16)


def parts_of(value, count):
    parts = []
    for _ in range(count):
        part = value.astype(jnp.bfloat16)
        parts.append(part)
        value = value - part.astype(jnp.float32)
    return parts


def dot32(a, b, dims):
    return lax.dot_general(a, b, dims, preferred_element_type=jnp.float32)


NN = (((1,), (0,)), ((), ()))


def stencil_tap(offset, gap):
    if offset == 0:
        along = jnp.where(gap == 0, -60.0, 0.0) + jnp.where(gap == 1, 16.0, 0.0)
        return along - jnp.where(gap == 2, 1.0, 0.0)
    weight = {1: 16.0, 2: -1.0}.get(abs(offset), 0.0)
    return jnp.where(gap == 0, weight, 0.0)


def gather_kernel(n, cells, snap_ref, weight_hbm, diff_hbm, flux_ref, sums_ref, rotation_ref,
                  weight_ref, diff_ref, pod, x_ref, parts, taps, part_sums, half, pieces, work, local_sem, grid_sem,
                  send_sem, recv_sem, halo_send, halo_recv, sum_send, sum_recv):
    me = lax.axis_index("gx")
    own, variables, _, cols = snap_ref.shape
    total, rows = pod.shape[0], pod.shape[2]

    barrier = pltpu.get_barrier_semaphore()

    def greet(k, carry):
        pl.semaphore_signal(
            barrier, inc=1, device_id={"gx": lax.rem(me + k, n)}, device_id_type=MESH
        )
        return carry

    lax.fori_loop(1, n, greet, 0)

    def own_copy(v):
        return pltpu.make_async_copy(
            snap_ref.at[:, v, pl.ds(me * rows, rows)],
            pod.at[pl.ds(me * own, own), v],
            local_sem.at[v],
        )

    def send_all(v):
        def send(k, carry):
            offset = lax.div(k, 2) + lax.rem(k, 2) * (n // 2)
            target = lax.rem(me + offset, n)
            pltpu.make_async_remote_copy(
                src_ref=snap_ref.at[:, v, pl.ds(target * rows, rows)],
                dst_ref=pod.at[pl.ds(me * own, own), v],
                send_sem=send_sem.at[v],
                recv_sem=recv_sem.at[v],
                device_id={"gx": target},
                device_id_type=MESH,
            ).start()
            return carry

        lax.fori_loop(1, n, send, 0)

    grid_copies = [
        pltpu.make_async_copy(weight_hbm, weight_ref, grid_sem.at[0]),
        pltpu.make_async_copy(diff_hbm, diff_ref, grid_sem.at[1]),
    ]
    for copy in grid_copies:
        copy.start()
    for v in range(variables):
        own_copy(v).start()
    pl.semaphore_wait(barrier, n - 1)
    ahead = min(2, variables)
    for v in range(ahead):
        send_all(v)

    part_sums[...] = jnp.zeros_like(part_sums)
    for copy in grid_copies:
        copy.wait()
    for k in range(PAIR + 4):
        for r in range(PAIR):
            gap = jnp.abs(iota((cols, cols), 0) - iota((cols, cols), 1))
            tap = stencil_tap(k - r - 2, gap)
            taps[k * cols : (k + 1) * cols, r * cols : (r + 1) * cols] = tap.astype(jnp.bfloat16)
    swap = swap_matrix(rows, PACK)

    def all_but_own(v, sem):
        piece = pod.at[pl.ds(0, total - own), v]
        return pltpu.make_async_copy(piece, piece, sem.at[v])

    def strip(v, first, count):
        return x_ref.at[v, :, pl.ds(first * cols, count * cols)]

    def to_low(v):
        return pltpu.make_async_remote_copy(
            src_ref=strip(v, 2, 2),
            dst_ref=strip(v, rows + 2, 2),
            send_sem=halo_send.at[0, v],
            recv_sem=halo_recv.at[0, v],
            device_id={"gx": jnp.maximum(me - 1, 0)},
            device_id_type=MESH,
        )

    def to_high(v):
        return pltpu.make_async_remote_copy(
            src_ref=strip(v, rows, 2),
            dst_ref=strip(v, 0, 2),
            send_sem=halo_send.at[1, v],
            recv_sem=halo_recv.at[1, v],
            device_id={"gx": jnp.minimum(me + 1, n - 1)},
            device_id_type=MESH,
        )

    def relayout(v):
        for g in range(0, total // PACK, 2):
            blocks = [
                pod[PACK * (g + h) : PACK * (g + h + 1), v].reshape(PACK * rows, cols)
                for h in range(2)
            ]
            turned = dot32(swap, jnp.concatenate(blocks, axis=1), NN).astype(jnp.bfloat16)
            for h in range(2):
                for at in range(rows):
                    x_ref[v, PACK * (g + h) : PACK * (g + h + 1), (at + 2) * cols : (at + 3) * cols] = (
                        turned[at * PACK : (at + 1) * PACK, h * cols : (h + 1) * cols]
                    )

    def accumulate(which, pairs):
        acc = dot32(*pairs[0], NT)
        for left, right in pairs[1:]:
            acc += dot32(left, right, NT)
        part_sums[which, 0] += acc[:, : total // 2]
        part_sums[which, 1] += acc[:, total // 2 :]

    def gram(v):
        for at in range(rows):
            field = x_ref[v, :, (at + 2) * cols : (at + 3) * cols].astype(jnp.float32)
            for p, part in enumerate(parts_of(field * weight_ref[at : at + 1, :], 3)):
                parts[p, :, at * cols : (at + 1) * cols] = part
        left = x_ref[v, :, 2 * cols : (rows + 2) * cols]
        accumulate(0, [(left, parts[p]) for p in range(3)])

    def halo_wait(v):
        @pl.when(me < n - 1)
        def _():
            to_low(v).wait_recv()
            to_high(v).wait_send()

        @pl.when(me > 0)
        def _():
            to_high(v).wait_recv()
            to_low(v).wait_send()

    def diffuse(v, first, last):
        for at in range(first, last, PAIR):
            window = x_ref[v, :, at * cols : (at + PAIR + 4) * cols]
            scale = jnp.concatenate(
                [diff_ref[v, at + r : at + r + 1, :] for r in range(PAIR)], axis=1
            )
            spread = dot32(window, taps[...], NN) * (scale / 12.0)
            for p, part in enumerate(parts_of(spread, 2)):
                flux_ref[v, p, :, at * cols : (at + PAIR) * cols] = part

    def project(v):
        accumulate(1, [(parts[0], flux_ref[v, 0]), (parts[0], flux_ref[v, 1]), (parts[1], flux_ref[v, 0])])

    @pl.loop(0, variables)
    def _(v):
        @pl.when(v > 0)
        def _():
            halo_wait(v - 1)
            diffuse(v - 1, 0, rows)
            project(v - 1)

        own_copy(v).wait()
        all_but_own(v, recv_sem).wait()
        relayout(v)

        @pl.when(me > 0)
        def _():
            to_low(v).start()

        @pl.when(me < n - 1)
        def _():
            to_high(v).start()

        @pl.when(me == 0)
        def _():
            x_ref[v, :, : 2 * cols] = jnp.zeros((total, 2 * cols), jnp.bfloat16)

        @pl.when(me == n - 1)
        def _():
            x_ref[v, :, (rows + 2) * cols :] = jnp.zeros((total, 2 * cols), jnp.bfloat16)

        @pl.when(v + ahead < variables)
        def _():
            send_all(v + ahead)

        gram(v)

    core, chip, chips = lax.rem(me, 2), lax.div(me, 2), n // 2
    share = total // chips
    partner = me + 1 - 2 * core

    mine = pl.ds(pl.multiple_of(chip * share, share), share)

    def remote(source, target, which, stage, device):
        return pltpu.make_async_remote_copy(
            src_ref=source,
            dst_ref=target,
            send_sem=sum_send.at[which, stage],
            recv_sem=sum_recv.at[which, stage],
            device_id={"gx": device},
            device_id_type=MESH,
        )

    def peer(k):
        return lax.rem(chip + k, chips)

    def pair_up(which):
        return remote(part_sums.at[which, 1 - core], half.at[which], which, 0, partner)

    def scatter(which):
        pair_up(which).wait()
        half[which] += part_sums[which, core]

        def send(k, carry):
            piece = half.at[which, pl.ds(peer(k) * share, share)]
            remote(piece, pieces.at[which, k - 1], which, 1, 2 * peer(k) + core).start()
            return carry

        lax.fori_loop(1, chips, send, 0)

    def spread_out(which):
        remote(pieces.at[which], pieces.at[which], which, 1, partner).wait()
        acc = half[which, mine, :]
        for k in range(chips - 1):
            acc += pieces[which, k]
        sums_ref[which, core, mine, :] = acc

        def send(k, carry):
            piece = sums_ref.at[which, core, mine]
            remote(piece, piece, which, 2, 2 * peer(k) + core).start()
            return carry

        lax.fori_loop(1, chips, send, 0)

    def hand_over(which):
        others = sums_ref.at[which, core, pl.ds(0, total - share)]
        remote(others, others, which, 2, partner).wait()
        done = sums_ref.at[which, core]
        remote(done, done, which, 3, partner).start()

    def finish(which):
        sent, got = sums_ref.at[which, core], sums_ref.at[which, 1 - core]
        remote(sent, sent, which, 3, partner).wait_send()
        remote(got, got, which, 3, partner).wait_recv()

    tail = variables - 1
    inner = rows // PAIR // 2 * PAIR
    pair_up(0).start()
    diffuse(tail, PAIR, inner)
    scatter(0)
    diffuse(tail, inner, rows - PAIR)
    halo_wait(tail)
    diffuse(tail, 0, PAIR)
    diffuse(tail, rows - PAIR, rows)
    project(tail)
    pair_up(1).start()
    spread_out(0)
    hand_over(0)
    finish(0)

    stages = {1: scatter, 3: spread_out, 5: hand_over, 7: finish}
    for step in factor(cells, sums_ref, rotation_ref, work):
        if step in stages:
            stages.pop(step)(1)
    for stage in stages.values():
        stage(1)

    for v in range(variables):
        all_but_own(v, send_sem).wait()


def factor(cells, sums_ref, rotation_ref, work):
    size = rotation_ref.shape[0]
    lanes = 128
    work[:, : size // 2] = sums_ref[0, 0] * (1.0 / cells)
    work[:, size // 2 : size] = sums_ref[0, 1] * (1.0 / cells)
    work[:, size:] = jnp.where(iota((size, size), 0) == iota((size, size), 1), 1.0, 0.0)
    rotation_ref[...] = jnp.zeros_like(rotation_ref)
    row = iota((PIVOTS, lanes), 0)
    lane = iota((PIVOTS, lanes), 1)
    for first in range(0, size, PIVOTS):
        last = first + PIVOTS
        group, shift = first // lanes * lanes, first % lanes
        stop = size + group + lanes
        block = work[first:last, group : group + lanes]
        if shift:
            block = pltpu.roll(block, lanes - shift, 1)
        block = jnp.where(lane < PIVOTS, block, jnp.where(lane == row + PIVOTS, 1.0, 0.0))
        for base in range(0, PIVOTS, PANEL):
            columns = [
                jnp.broadcast_to(block[:, k : k + 1], (PIVOTS, lanes))
                for k in range(base, base + PANEL)
            ]
            for j in range(PANEL):
                k = base + j
                factor_of = jnp.where(row > k, columns[j] * (1.0 / columns[j][k : k + 1, :]), 0.0)
                for i in range(j + 1, PANEL):
                    columns[i] = columns[i] - factor_of * columns[i][k : k + 1, :]
                block = block - factor_of * block[k : k + 1, :]
        pivots = jnp.sum(jnp.where(lane == row, block, 0.0), axis=1, keepdims=True)
        inverse = pltpu.roll(block, lanes - PIVOTS, 1) / jnp.sqrt(pivots)
        stripe = jnp.dot(
            inverse[:, :PIVOTS],
            work[first:last, group:stop],
            precision=HIGHEST,
            preferred_element_type=jnp.float32,
        )
        rotation_ref[first:last, : group + lanes] = stripe[:, size - group :]
        if last < size:
            low = last // lanes * lanes
            work[low:, group:stop] -= lax.dot_general(
                stripe[:, low - group : size - group],
                stripe,
                TN,
                precision=HIGHEST,
                preferred_element_type=jnp.float32,
            )
        yield first // PIVOTS


def gather(n, cells, snapshots, cell_weights, diffusivity):
    own, variables, _, cols = snapshots.shape
    rows = cell_weights.shape[0]
    total = own * n
    vmem = pl.BlockSpec(memory_space=pltpu.VMEM)
    chips = n // 2
    dma = pltpu.SemaphoreType.DMA
    return pl.pallas_call(
        functools.partial(gather_kernel, n, float(cells)),
        out_shape=(
            pltpu.VMEM((variables, 2, total, rows * cols), jnp.bfloat16),
            pltpu.VMEM((2, 2, total, total // 2), jnp.float32),
            pltpu.VMEM((total, total), jnp.float32),
        ),
        in_specs=[pl.BlockSpec(memory_space=pltpu.HBM)] * 3,
        out_specs=(vmem, vmem, vmem),
        scratch_shapes=[
            pltpu.VMEM(cell_weights.shape, jnp.float32),
            pltpu.VMEM(diffusivity.shape, jnp.float32),
            pltpu.VMEM((total, variables, rows, cols), jnp.bfloat16),
            pltpu.VMEM((variables, total, (rows + 4) * cols), jnp.bfloat16),
            pltpu.VMEM((3, total, rows * cols), jnp.bfloat16),
            pltpu.VMEM(((PAIR + 4) * cols, PAIR * cols), jnp.bfloat16),
            pltpu.VMEM((2, 2, total, total // 2), jnp.float32),
            pltpu.VMEM((2, total, total // 2), jnp.float32),
            pltpu.VMEM((2, chips - 1, total // chips, total // 2), jnp.float32),
            pltpu.VMEM((total, 2 * total), jnp.float32),
            dma((variables,)),
            dma((2,)),
            dma((variables,)),
            dma((variables,)),
            dma((2, variables)),
            dma((2, variables)),
            dma((2, 4)),
            dma((2, 4)),
        ],
        compiler_params=pltpu.CompilerParams(
            collective_id=0, has_side_effects=True, vmem_limit_bytes=GATHER_VMEM
        ),
        name="gather",
    )(snapshots, cell_weights, diffusivity)


def modes_kernel(cells, rotation_ref, sums_ref, flux_ref, out_ref, reduced_ref, turned, staged, out_sem):
    variables, total, rows, cols = staged.shape
    wide, fine = parts_of(rotation_ref[...], 2)
    swap = swap_matrix(PACK, rows)

    def out_copy(v):
        return pltpu.make_async_copy(staged.at[v], out_ref.at[:, v], out_sem.at[v])

    @pl.loop(0, variables)
    def _(v):
        for at in range(0, rows, PAIR):
            lanes = slice(at * cols, (at + PAIR) * cols)
            top, rest = flux_ref[v, 0, :, lanes], flux_ref[v, 1, :, lanes]
            acc = dot32(wide, top, NN) + dot32(wide, rest, NN) + dot32(fine, top, NN)
            for r in range(PAIR):
                turned[at + r] = acc[:, r * cols : (r + 1) * cols].astype(jnp.bfloat16)
        for g in range(0, total // PACK, 2):
            blocks = [
                turned[:, PACK * (g + h) : PACK * (g + h + 1), :].reshape(rows * PACK, cols)
                for h in range(2)
            ]
            done = dot32(swap, jnp.concatenate(blocks, axis=1), NN).astype(jnp.bfloat16)
            for h in range(2):
                staged[v, PACK * (g + h) : PACK * (g + h + 1)] = done[
                    :, h * cols : (h + 1) * cols
                ].reshape(PACK, rows, cols)
        out_copy(v).start()

    rotation = rotation_ref[...]
    cross = jnp.concatenate([sums_ref[1, 0], sums_ref[1, 1]], axis=1) * (1.0 / cells)
    product = jnp.dot(rotation, cross, precision=HIGHEST, preferred_element_type=jnp.float32)
    reduced_ref[...] = lax.dot_general(
        product, rotation, NT, precision=HIGHEST, preferred_element_type=jnp.float32
    )
    for v in range(variables):
        out_copy(v).wait()


def modes(cells, rotation, sums, flux, rows):
    variables, _, total, width = flux.shape
    cols = width // rows
    vmem = pl.BlockSpec(memory_space=pltpu.VMEM)
    return pl.pallas_call(
        functools.partial(modes_kernel, float(cells)),
        out_shape=(
            jax.ShapeDtypeStruct((total, variables, rows, cols), jnp.bfloat16),
            jax.ShapeDtypeStruct((total, total), jnp.float32),
        ),
        in_specs=[vmem] * 3,
        out_specs=(pl.BlockSpec(memory_space=pl.ANY), vmem),
        scratch_shapes=[
            pltpu.VMEM((rows, total, cols), jnp.bfloat16),
            pltpu.VMEM((variables, total, rows, cols), jnp.bfloat16),
            pltpu.SemaphoreType.DMA((variables,)),
        ],
        compiler_params=pltpu.CompilerParams(vmem_limit_bytes=MODES_VMEM),
        name="modes",
    )(rotation, sums, flux)


def on_device(n, snapshots, cell_weights, diffusivity):
    variables, rows, cols = diffusivity.shape
    cells = variables * rows * cols * n
    flux, sums, rotation = gather(n, cells, snapshots, cell_weights, diffusivity)
    return modes(cells, rotation, sums, flux, rows)


def solution(mesh):
    in_specs = (
        P("gx", None, "groups", None),
        P(("groups", "gx"), None),
        P(None, ("groups", "gx"), None),
    )
    out_specs = (P(None, None, ("groups", "gx"), None), P("groups", None))
    return jax.shard_map(
        functools.partial(on_device, mesh.shape["gx"]),
        mesh=mesh, in_specs=in_specs, out_specs=out_specs, check_vma=False,
    )
```

```python
import functools

import jax
import jax.numpy as jnp
from jax import lax
from jax.experimental import pallas as pl
from jax.experimental.pallas import tpu as pltpu
from jax.sharding import PartitionSpec as P

MESH = pl.DeviceIdType.MESH
HIGHEST = lax.Precision.HIGHEST
NT = (((1,), (1,)), ((), ()))
TN = (((0,), (0,)), ((), ()))
NN = (((1,), (0,)), ((), ()))
PACK = 16
PIVOTS = 64
PANEL = 16
SUBLANES = 8
PAIR = 2
GATHER_VMEM = 54 * 2**20
MODES_VMEM = 40 * 2**20


def iota(shape, dim):
    return lax.broadcasted_iota(jnp.int32, shape, dim)


def swap_matrix(outer, inner):
    size = outer * inner
    row, col = iota((size, size), 0), iota((size, size), 1)
    source = lax.rem(row, inner) * outer + lax.div(row, inner)
    return jnp.where(col == source, 1.0, 0.0).astype(jnp.bfloat16)


def parts_of(value, count):
    parts = []
    for _ in range(count):
        part = value.astype(jnp.bfloat16)
        parts.append(part)
        value = value - part.astype(jnp.float32)
    return parts


def dot32(a, b, dims):
    return lax.dot_general(a, b, dims, preferred_element_type=jnp.float32)


def stencil_tap(offset, gap):
    if offset == 0:
        along = jnp.where(gap == 0, -60.0, 0.0) + jnp.where(gap == 1, 16.0, 0.0)
        return along - jnp.where(gap == 2, 1.0, 0.0)
    weight = {1: 16.0, 2: -1.0}.get(abs(offset), 0.0)
    return jnp.where(gap == 0, weight, 0.0)


def gather_kernel(n, cells, snap_ref, weight_hbm, diff_hbm, flux_ref, sums_ref, rotation_ref,
                  weight_ref, diff_ref, pod, x_ref, parts, taps, part_sums, packed, gram_half,
                  cross_half, gram_pieces, cross_pieces, diagonals, gram_ref, work, local_sem,
                  grid_sem, send_sem, recv_sem, halo_send, halo_recv, sum_send, sum_recv):
    me = lax.axis_index("gx")
    own, variables, _, cols = snap_ref.shape
    total, rows = pod.shape[0], pod.shape[2]

    barrier = pltpu.get_barrier_semaphore()

    def greet(k, carry):
        pl.semaphore_signal(
            barrier, inc=1, device_id={"gx": lax.rem(me + k, n)}, device_id_type=MESH
        )
        return carry

    lax.fori_loop(1, n, greet, 0)

    def own_copy(v):
        return pltpu.make_async_copy(
            snap_ref.at[:, v, pl.ds(me * rows, rows)],
            pod.at[pl.ds(me * own, own), v],
            local_sem.at[v],
        )

    def send_all(v):
        def send(k, carry):
            offset = lax.div(k, 2) + lax.rem(k, 2) * (n // 2)
            target = lax.rem(me + offset, n)
            pltpu.make_async_remote_copy(
                src_ref=snap_ref.at[:, v, pl.ds(target * rows, rows)],
                dst_ref=pod.at[pl.ds(me * own, own), v],
                send_sem=send_sem.at[v],
                recv_sem=recv_sem.at[v],
                device_id={"gx": target},
                device_id_type=MESH,
            ).start()
            return carry

        lax.fori_loop(1, n, send, 0)

    grid_copies = [
        pltpu.make_async_copy(weight_hbm, weight_ref, grid_sem.at[0]),
        pltpu.make_async_copy(diff_hbm, diff_ref, grid_sem.at[1]),
    ]
    for copy in grid_copies:
        copy.start()
    for v in range(variables):
        own_copy(v).start()
    pl.semaphore_wait(barrier, n - 1)
    ahead = min(2, variables)
    for v in range(ahead):
        send_all(v)

    part_sums[...] = jnp.zeros_like(part_sums)
    rotation_ref[...] = jnp.zeros_like(rotation_ref)
    work[:, total:] = jnp.where(iota((total, total), 0) == iota((total, total), 1), 1.0, 0.0)
    for copy in grid_copies:
        copy.wait()
    for k in range(PAIR + 4):
        for r in range(PAIR):
            gap = jnp.abs(iota((cols, cols), 0) - iota((cols, cols), 1))
            tap = stencil_tap(k - r - 2, gap)
            taps[k * cols : (k + 1) * cols, r * cols : (r + 1) * cols] = tap.astype(jnp.bfloat16)
    swap = swap_matrix(rows, PACK)

    def all_but_own(v, sem):
        piece = pod.at[pl.ds(0, total - own), v]
        return pltpu.make_async_copy(piece, piece, sem.at[v])

    def strip(v, first, count):
        return x_ref.at[v, :, pl.ds(first * cols, count * cols)]

    def to_low(v):
        return pltpu.make_async_remote_copy(
            src_ref=strip(v, 2, 2),
            dst_ref=strip(v, rows + 2, 2),
            send_sem=halo_send.at[0, v],
            recv_sem=halo_recv.at[0, v],
            device_id={"gx": jnp.maximum(me - 1, 0)},
            device_id_type=MESH,
        )

    def to_high(v):
        return pltpu.make_async_remote_copy(
            src_ref=strip(v, rows, 2),
            dst_ref=strip(v, 0, 2),
            send_sem=halo_send.at[1, v],
            recv_sem=halo_recv.at[1, v],
            device_id={"gx": jnp.minimum(me + 1, n - 1)},
            device_id_type=MESH,
        )

    def relayout(v):
        for g in range(0, total // PACK, 2):
            blocks = [
                pod[PACK * (g + h) : PACK * (g + h + 1), v].reshape(PACK * rows, cols)
                for h in range(2)
            ]
            turned = dot32(swap, jnp.concatenate(blocks, axis=1), NN).astype(jnp.bfloat16)
            for h in range(2):
                for at in range(rows):
                    x_ref[v, PACK * (g + h) : PACK * (g + h + 1), (at + 2) * cols : (at + 3) * cols] = (
                        turned[at * PACK : (at + 1) * PACK, h * cols : (h + 1) * cols]
                    )

    def accumulate(which, pairs):
        acc = dot32(*pairs[0], NT)
        for left, right in pairs[1:]:
            acc += dot32(left, right, NT)
        part_sums[which, 0] += acc[:, : total // 2]
        part_sums[which, 1] += acc[:, total // 2 :]

    def slot(v):
        return lax.rem(v, 2)

    def gram(v):
        for at in range(rows):
            field = x_ref[v, :, (at + 2) * cols : (at + 3) * cols].astype(jnp.float32)
            for p, part in enumerate(parts_of(field * weight_ref[at : at + 1, :], 3)):
                parts[slot(v), p, :, at * cols : (at + 1) * cols] = part
        left = x_ref[v, :, 2 * cols : (rows + 2) * cols]
        accumulate(0, [(left, parts[slot(v), p]) for p in range(3)])

    def halo_wait(v):
        @pl.when(me < n - 1)
        def _():
            to_low(v).wait_recv()
            to_high(v).wait_send()

        @pl.when(me > 0)
        def _():
            to_high(v).wait_recv()
            to_low(v).wait_send()

    def diffuse(v, first, last):
        for at in range(first, last, PAIR):
            window = x_ref[v, :, at * cols : (at + PAIR + 4) * cols]
            scale = jnp.concatenate(
                [diff_ref[v, at + r : at + r + 1, :] for r in range(PAIR)], axis=1
            )
            spread = dot32(window, taps[...], NN) * (scale / 12.0)
            for p, part in enumerate(parts_of(spread, 2)):
                flux_ref[v, p, :, at * cols : (at + PAIR) * cols] = part

    def project(v):
        halo_wait(v)
        diffuse(v, 0, PAIR)
        diffuse(v, rows - PAIR, rows)
        wide, fine = parts[slot(v), 0], parts[slot(v), 1]
        accumulate(1, [(wide, flux_ref[v, 0]), (wide, flux_ref[v, 1]), (fine, flux_ref[v, 0])])

    def arrive(v):
        own_copy(v).wait()
        all_but_own(v, recv_sem).wait()
        relayout(v)

        @pl.when(me > 0)
        def _():
            to_low(v).start()

        @pl.when(me < n - 1)
        def _():
            to_high(v).start()

        @pl.when(me == 0)
        def _():
            x_ref[v, :, : 2 * cols] = jnp.zeros((total, 2 * cols), jnp.bfloat16)

        @pl.when(me == n - 1)
        def _():
            x_ref[v, :, (rows + 2) * cols :] = jnp.zeros((total, 2 * cols), jnp.bfloat16)

    tail = variables - 1

    @pl.loop(0, tail)
    def _(v):
        arrive(v)

        @pl.when(v + ahead < variables)
        def _():
            send_all(v + ahead)

        @pl.when(v > 0)
        def _():
            project(v - 1)

        gram(v)
        diffuse(v, PAIR, rows - PAIR)

    core, chip, chips = lax.rem(me, 2), lax.div(me, 2), n // 2
    partner = me + 1 - 2 * core
    lanes = total // 2
    extents = (lanes, total)
    shares = tuple(max(extent // chips, SUBLANES) for extent in extents)
    owners = tuple(extent // share for extent, share in zip(extents, shares))
    given = (packed, part_sums.at[1])
    halves = (gram_half, cross_half)
    pieces = (gram_pieces, cross_pieces)
    sums = (gram_ref, sums_ref)

    def remote(source, target, which, stage, device):
        return pltpu.make_async_remote_copy(
            src_ref=source,
            dst_ref=target,
            send_sem=sum_send.at[which, stage],
            recv_sem=sum_recv.at[which, stage],
            device_id={"gx": device},
            device_id_type=MESH,
        )

    def ledger(count, which, stage):
        ref = sums_ref.at[pl.ds(0, count)]
        return remote(ref, ref, which, stage, partner)

    def peer(k):
        return lax.rem(chip + k, chips)

    def is_owner(which, index, body, other=None):
        if owners[which] == chips:
            body()
            return
        pl.when(index < owners[which])(body)
        if other is not None:
            pl.when(index >= owners[which])(other)

    def mine(which, base):
        share = shares[which]
        return pl.ds(pl.multiple_of(base + chip * share, SUBLANES), share)

    def pack():
        low, high = part_sums[0, 0, :lanes], part_sums[0, 1, lanes:]
        row, lane = iota((lanes, lanes), 0), iota((lanes, lanes), 1)
        packed[0, :lanes] = part_sums[0, 1, :lanes]
        packed[1, :lanes] = jnp.where(row >= lane, low, high)
        diagonal = jnp.sum(jnp.where(row == lane, high, 0.0), axis=0, keepdims=True)
        for h in range(2):
            packed[h, lanes:] = jnp.broadcast_to(diagonal, (SUBLANES, lanes))

    def pair_up(which):
        return remote(given[which].at[1 - core], halves[which], which, 0, partner)

    def scatter(which):
        pair_up(which).wait()
        half = halves[which]
        half[...] += given[which][core]
        share = shares[which]

        def send(k, carry):
            def start():
                piece = half.at[pl.ds(pl.multiple_of(peer(k) * share, SUBLANES), share)]
                remote(piece, pieces[which].at[k - 1], which, 1, 2 * peer(k) + core).start()

            is_owner(which, peer(k), start)
            if which == 0:
                remote(
                    half.at[pl.ds(lanes, SUBLANES)], diagonals.at[chip], 0, 3, 2 * peer(k) + core
                ).start()
            return carry

        lax.fori_loop(1, chips, send, 0, unroll=True)
        if which == 0:
            diagonals[chip] = half[lanes:]

    def spread_out(which):
        share, half = shares[which], halves[which]

        def owned():
            ledger((owners[which] - 1) * share, which, 1).wait_send()
            remote(pieces[which], pieces[which], which, 1, partner).wait_recv()
            acc = half[mine(which, 0), :]
            for k in range(chips - 1):
                acc += pieces[which][k]
            place = mine(which, core * extents[which])
            sums[which][place, :] = acc

            def send(j, carry):
                k = 1 + lax.rem(n // 2 - 1 + j, n - 1)
                piece = sums[which].at[place]
                remote(piece, piece, which, 2, lax.rem(me + k, n)).start()
                return carry

            lax.fori_loop(0, n - 1, send, 0, unroll=True)

        def others():
            ledger(owners[which] * share, which, 1).wait_send()

        is_owner(which, chip, owned, others)

    def finish(which):
        share = shares[which]
        full = 2 * extents[which]

        def owned():
            got = sums[which].at[pl.ds(0, full - share)]
            remote(got, got, which, 2, partner).wait_recv()
            ledger((n - 1) * share, which, 2).wait_send()

        def others():
            remote(sums[which], sums[which], which, 2, partner).wait_recv()

        is_owner(which, chip, owned, others)

    def unpack():
        others = diagonals.at[pl.ds(0, chips - 1)]
        remote(others, others, 0, 3, partner).wait()
        scale = 1.0 / cells
        diagonal = diagonals[0]
        for k in range(1, chips):
            diagonal += diagonals[k]
        mixed = gram_ref[lanes:]
        turned = mixed.T
        row, lane = iota((lanes, lanes), 0), iota((lanes, lanes), 1)
        work[:lanes, :lanes] = jnp.where(row >= lane, mixed, turned) * scale
        work[:lanes, lanes:total] = gram_ref[:lanes] * scale
        high = jnp.where(row == lane, diagonal[:1], jnp.where(row < lane, mixed, turned))
        work[lanes:, lanes:total] = high * scale

    arrive(tail)
    gram(tail)
    pack()
    pair_up(0).start()
    if tail > 0:
        project(tail - 1)
    scatter(0)
    diffuse(tail, PAIR, rows - PAIR)
    project(tail)
    pair_up(1).start()
    spread_out(0)
    scatter(1)
    finish(0)
    unpack()

    for step in factor(work, rotation_ref):
        if step == 0:
            spread_out(1)
    finish(1)

    for v in range(variables):
        all_but_own(v, send_sem).wait()


def dot_exact(a, b, dims):
    return lax.dot_general(a, b, dims, precision=HIGHEST, preferred_element_type=jnp.float32)


def eliminate(block, base):
    count, lanes = block.shape
    row = iota((count, lanes), 0)
    columns = [
        jnp.broadcast_to(block[:, k : k + 1], (count, lanes)) for k in range(base, base + PANEL)
    ]
    for k in range(0, PANEL, 2):
        one, two = columns[k], columns[k + 1]
        a, b, d = one[k : k + 1], one[k + 1 : k + 2], two[k + 1 : k + 2]
        det = a * d - b * b
        inverse_a, inverse_det = 1.0 / a, 1.0 / det
        below = row > k + 1
        of_one = jnp.where(
            below, (one * d - two * b) * inverse_det, jnp.where(row == k + 1, b * inverse_a, 0.0)
        )
        of_two = jnp.where(below, (two * a - one * b) * inverse_det, 0.0)
        for i in range(k + 2, PANEL):
            column = columns[i]
            columns[i] = column - of_one * column[k : k + 1] - of_two * column[k + 1 : k + 2]
        block = block - of_one * block[k : k + 1] - of_two * block[k + 1 : k + 2]
    return block


def factor(work, rotation_ref):
    size, lanes = rotation_ref.shape[0], 128
    row = iota((PIVOTS, lanes), 0)
    lane = iota((PIVOTS, lanes), 1)

    def cut(rows, first):
        group, shift = first // lanes * lanes, first % lanes
        block = work[rows : rows + PIVOTS, group : group + lanes]
        return pltpu.roll(block, lanes - shift, 1) if shift else block

    ahead = cut(0, 0)
    for first in range(0, size, PIVOTS):
        last = first + PIVOTS
        group = first // lanes * lanes
        stop = size + group + lanes
        block = jnp.where(lane < PIVOTS, ahead, jnp.where(lane == row + PIVOTS, 1.0, 0.0))
        done = []
        for base in range(0, PIVOTS, PANEL):
            block = eliminate(block, base)
            done.append(block[:PANEL])
            block = block[PANEL:]
        block = jnp.concatenate(done, axis=0)
        pivots = jnp.sum(jnp.where(lane == row, block, 0.0), axis=1, keepdims=True)
        inverse = pltpu.roll(block, lanes - PIVOTS, 1) / jnp.sqrt(pivots)
        inverse = inverse[:, :PIVOTS]
        if last < size:
            side = dot_exact(inverse, cut(first, last), NN)
            ahead = cut(last, last) - dot_exact(side[:, :PIVOTS], side, TN)
        stripe = dot_exact(inverse, work[first:last, group:stop], NN)
        rotation_ref[first:last, : group + lanes] = stripe[:, size - group :]
        if last < size:
            low = last // lanes * lanes
            work[low:, low:stop] -= dot_exact(
                stripe[:, low - group : size - group], stripe[:, low - group :], TN
            )
        yield first // PIVOTS


def gather(n, cells, snapshots, cell_weights, diffusivity):
    own, variables, _, cols = snapshots.shape
    rows = cell_weights.shape[0]
    total = own * n
    vmem = pl.BlockSpec(memory_space=pltpu.VMEM)
    chips, lanes = n // 2, total // 2
    dma = pltpu.SemaphoreType.DMA
    return pl.pallas_call(
        functools.partial(gather_kernel, n, float(cells)),
        out_shape=(
            pltpu.VMEM((variables, 2, total, rows * cols), jnp.bfloat16),
            pltpu.VMEM((2 * total, total // 2), jnp.float32),
            pltpu.VMEM((total, total), jnp.float32),
        ),
        in_specs=[pl.BlockSpec(memory_space=pltpu.HBM)] * 3,
        out_specs=(vmem, vmem, vmem),
        scratch_shapes=[
            pltpu.VMEM(cell_weights.shape, jnp.float32),
            pltpu.VMEM(diffusivity.shape, jnp.float32),
            pltpu.VMEM((total, variables, rows, cols), jnp.bfloat16),
            pltpu.VMEM((variables, total, (rows + 4) * cols), jnp.bfloat16),
            pltpu.VMEM((2, 3, total, rows * cols), jnp.bfloat16),
            pltpu.VMEM(((PAIR + 4) * cols, PAIR * cols), jnp.bfloat16),
            pltpu.VMEM((2, 2, total, total // 2), jnp.float32),
            pltpu.VMEM((2, lanes + SUBLANES, lanes), jnp.float32),
            pltpu.VMEM((lanes + SUBLANES, lanes), jnp.float32),
            pltpu.VMEM((total, lanes), jnp.float32),
            pltpu.VMEM((chips - 1, max(lanes // chips, SUBLANES), lanes), jnp.float32),
            pltpu.VMEM((chips - 1, max(total // chips, SUBLANES), lanes), jnp.float32),
            pltpu.VMEM((chips, SUBLANES, lanes), jnp.float32),
            pltpu.VMEM((total, lanes), jnp.float32),
            pltpu.VMEM((total, 2 * total), jnp.float32),
            dma((variables,)),
            dma((2,)),
            dma((variables,)),
            dma((variables,)),
            dma((2, variables)),
            dma((2, variables)),
            dma((2, 4)),
            dma((2, 4)),
        ],
        compiler_params=pltpu.CompilerParams(
            collective_id=0, has_side_effects=True, vmem_limit_bytes=GATHER_VMEM
        ),
        name="gather",
    )(snapshots, cell_weights, diffusivity)


def modes_kernel(cells, rotation_ref, sums_ref, flux_ref, out_ref, reduced_ref, turned, staged, out_sem):
    variables, total, rows, cols = staged.shape
    wide, fine = parts_of(rotation_ref[...], 2)
    swap = swap_matrix(PACK, rows)

    def out_copy(v):
        return pltpu.make_async_copy(staged.at[v], out_ref.at[:, v], out_sem.at[v])

    @pl.loop(0, variables)
    def _(v):
        for at in range(0, rows, PAIR):
            lanes = slice(at * cols, (at + PAIR) * cols)
            top, rest = flux_ref[v, 0, :, lanes], flux_ref[v, 1, :, lanes]
            acc = dot32(wide, top, NN) + dot32(wide, rest, NN) + dot32(fine, top, NN)
            for r in range(PAIR):
                turned[at + r] = acc[:, r * cols : (r + 1) * cols].astype(jnp.bfloat16)
        for g in range(0, total // PACK, 2):
            blocks = [
                turned[:, PACK * (g + h) : PACK * (g + h + 1), :].reshape(rows * PACK, cols)
                for h in range(2)
            ]
            done = dot32(swap, jnp.concatenate(blocks, axis=1), NN).astype(jnp.bfloat16)
            for h in range(2):
                staged[v, PACK * (g + h) : PACK * (g + h + 1)] = done[
                    :, h * cols : (h + 1) * cols
                ].reshape(PACK, rows, cols)
        out_copy(v).start()

    rotation = rotation_ref[...]
    cross = jnp.concatenate([sums_ref[:total], sums_ref[total:]], axis=1) * (1.0 / cells)
    product = jnp.dot(rotation, cross, precision=HIGHEST, preferred_element_type=jnp.float32)
    reduced_ref[...] = lax.dot_general(
        product, rotation, NT, precision=HIGHEST, preferred_element_type=jnp.float32
    )
    for v in range(variables):
        out_copy(v).wait()


def modes(cells, rotation, sums, flux, rows):
    variables, _, total, width = flux.shape
    cols = width // rows
    vmem = pl.BlockSpec(memory_space=pltpu.VMEM)
    return pl.pallas_call(
        functools.partial(modes_kernel, float(cells)),
        out_shape=(
            jax.ShapeDtypeStruct((total, variables, rows, cols), jnp.bfloat16),
            jax.ShapeDtypeStruct((total, total), jnp.float32),
        ),
        in_specs=[vmem] * 3,
        out_specs=(pl.BlockSpec(memory_space=pl.ANY), vmem),
        scratch_shapes=[
            pltpu.VMEM((rows, total, cols), jnp.bfloat16),
            pltpu.VMEM((variables, total, rows, cols), jnp.bfloat16),
            pltpu.SemaphoreType.DMA((variables,)),
        ],
        compiler_params=pltpu.CompilerParams(vmem_limit_bytes=MODES_VMEM),
        name="modes",
    )(rotation, sums, flux)


def on_device(n, snapshots, cell_weights, diffusivity):
    variables, rows, cols = diffusivity.shape
    cells = variables * rows * cols * n
    flux, sums, rotation = gather(n, cells, snapshots, cell_weights, diffusivity)
    return modes(cells, rotation, sums, flux, rows)


def solution(mesh):
    in_specs = (
        P("gx", None, "groups", None),
        P(("groups", "gx"), None),
        P(None, ("groups", "gx"), None),
    )
    out_specs = (P(None, None, ("groups", "gx"), None), P("groups", None))
    return jax.shard_map(
        functools.partial(on_device, mesh.shape["gx"]),
        mesh=mesh, in_specs=in_specs, out_specs=out_specs, check_vma=False,
    )
```

```python
import functools

import jax
import jax.numpy as jnp
from jax import lax
from jax.experimental import pallas as pl
from jax.experimental.pallas import tpu as pltpu
from jax.sharding import PartitionSpec as P

MESH = pl.DeviceIdType.MESH
HIGHEST = lax.Precision.HIGHEST
NT = (((1,), (1,)), ((), ()))
TN = (((0,), (0,)), ((), ()))
NN = (((1,), (0,)), ((), ()))
PACK = 16
PIVOTS = 64
PANEL = 16
SUBLANES = 8
PAIR = 2
GATHER_VMEM = 54 * 2**20
FINISH_VMEM = 40 * 2**20


def iota(shape, dim):
    return lax.broadcasted_iota(jnp.int32, shape, dim)


def swap_matrix(outer, inner):
    size = outer * inner
    row, col = iota((size, size), 0), iota((size, size), 1)
    source = lax.rem(row, inner) * outer + lax.div(row, inner)
    return jnp.where(col == source, 1.0, 0.0).astype(jnp.bfloat16)


def parts_of(value, count):
    parts = []
    for _ in range(count):
        part = value.astype(jnp.bfloat16)
        parts.append(part)
        value = value - part.astype(jnp.float32)
    return parts


def dot32(a, b, dims):
    return lax.dot_general(a, b, dims, preferred_element_type=jnp.float32)


def stencil_tap(offset, gap):
    if offset == 0:
        along = jnp.where(gap == 0, -60.0, 0.0) + jnp.where(gap == 1, 16.0, 0.0)
        return along - jnp.where(gap == 2, 1.0, 0.0)
    weight = {1: 16.0, 2: -1.0}.get(abs(offset), 0.0)
    return jnp.where(gap == 0, weight, 0.0)


def gather_kernel(n, cells, snap_ref, weight_hbm, diff_hbm, field_ref, sums_ref, rotation_ref,
                  turned, flux_ref, weight_ref, diff_ref, pod, x_ref, parts, taps, part_sums, packed, gram_half,
                  cross_half, gram_pieces, cross_pieces, diagonals, gram_ref, work, local_sem,
                  grid_sem, send_sem, recv_sem, halo_send, halo_recv, sum_send, sum_recv):
    me = lax.axis_index("gx")
    own, variables, _, cols = snap_ref.shape
    total, rows = pod.shape[0], pod.shape[2]

    barrier = pltpu.get_barrier_semaphore()

    def greet(k, carry):
        pl.semaphore_signal(
            barrier, inc=1, device_id={"gx": lax.rem(me + k, n)}, device_id_type=MESH
        )
        return carry

    lax.fori_loop(1, n, greet, 0)

    def own_copy(v):
        return pltpu.make_async_copy(
            snap_ref.at[:, v, pl.ds(me * rows, rows)],
            pod.at[pl.ds(me * own, own), v],
            local_sem.at[v],
        )

    def member(k):
        return me ^ k if n & (n - 1) == 0 else lax.rem(me + k, n)

    def send(v, k):
        target = member(k)
        pltpu.make_async_remote_copy(
            src_ref=snap_ref.at[:, v, pl.ds(target * rows, rows)],
            dst_ref=pod.at[pl.ds(me * own, own), v],
            send_sem=send_sem.at[v],
            recv_sem=recv_sem.at[v],
            device_id={"gx": target},
            device_id_type=MESH,
        ).start()

    def send_phase(v, near):
        for i in range(n - n // 2):
            send(v, n // 2 + i)
            if i + 1 < n // 2:
                for w in near:
                    send(w, i + 1)

    grid_copies = [
        pltpu.make_async_copy(weight_hbm, weight_ref, grid_sem.at[0]),
        pltpu.make_async_copy(diff_hbm, diff_ref, grid_sem.at[1]),
    ]
    for copy in grid_copies:
        copy.start()
    for v in range(variables):
        own_copy(v).start()
    pl.semaphore_wait(barrier, n - 1)
    ahead = min(2, variables)
    each = -(-variables // ahead)
    for v in range(ahead):
        send_phase(v, range(v * each, min((v + 1) * each, variables)))

    part_sums[...] = jnp.zeros_like(part_sums)
    rotation_ref[...] = jnp.zeros_like(rotation_ref)
    work[:, total:] = jnp.where(iota((total, total), 0) == iota((total, total), 1), 1.0, 0.0)
    for copy in grid_copies:
        copy.wait()
    for k in range(PAIR + 4):
        for r in range(PAIR):
            gap = jnp.abs(iota((cols, cols), 0) - iota((cols, cols), 1))
            tap = stencil_tap(k - r - 2, gap)
            taps[k * cols : (k + 1) * cols, r * cols : (r + 1) * cols] = tap.astype(jnp.bfloat16)
    swap = swap_matrix(rows, PACK)

    def all_but_own(v, sem):
        piece = pod.at[pl.ds(0, total - own), v]
        return pltpu.make_async_copy(piece, piece, sem.at[v])

    def strip(v, first, count):
        return x_ref.at[v, :, pl.ds(first * cols, count * cols)]

    def to_low(v):
        return pltpu.make_async_remote_copy(
            src_ref=strip(v, 2, 2),
            dst_ref=strip(v, rows + 2, 2),
            send_sem=halo_send.at[0, v],
            recv_sem=halo_recv.at[0, v],
            device_id={"gx": jnp.maximum(me - 1, 0)},
            device_id_type=MESH,
        )

    def to_high(v):
        return pltpu.make_async_remote_copy(
            src_ref=strip(v, rows, 2),
            dst_ref=strip(v, 0, 2),
            send_sem=halo_send.at[1, v],
            recv_sem=halo_recv.at[1, v],
            device_id={"gx": jnp.minimum(me + 1, n - 1)},
            device_id_type=MESH,
        )

    def relayout(v):
        for g in range(0, total // PACK, 2):
            blocks = [
                pod[PACK * (g + h) : PACK * (g + h + 1), v].reshape(PACK * rows, cols)
                for h in range(2)
            ]
            turned = dot32(swap, jnp.concatenate(blocks, axis=1), NN).astype(jnp.bfloat16)
            for h in range(2):
                for at in range(rows):
                    x_ref[v, PACK * (g + h) : PACK * (g + h + 1), (at + 2) * cols : (at + 3) * cols] = (
                        turned[at * PACK : (at + 1) * PACK, h * cols : (h + 1) * cols]
                    )

    def accumulate(which, pairs):
        acc = dot32(*pairs[0], NT)
        for left, right in pairs[1:]:
            acc += dot32(left, right, NT)
        part_sums[which, 0] += acc[:, : total // 2]
        part_sums[which, 1] += acc[:, total // 2 :]

    def slot(v):
        return lax.rem(v, 2)

    def gram(v):
        for at in range(rows):
            field = x_ref[v, :, (at + 2) * cols : (at + 3) * cols].astype(jnp.float32)
            for p, part in enumerate(parts_of(field * weight_ref[at : at + 1, :], 3)):
                parts[slot(v), p, :, at * cols : (at + 1) * cols] = part
        left = x_ref[v, :, 2 * cols : (rows + 2) * cols]
        accumulate(0, [(left, parts[slot(v), p]) for p in range(3)])

    def halo_wait(v):
        @pl.when(me < n - 1)
        def _():
            to_low(v).wait_recv()
            to_high(v).wait_send()

        @pl.when(me > 0)
        def _():
            to_high(v).wait_recv()
            to_low(v).wait_send()

    def diffuse(v, first, last):
        for at in range(first, last, PAIR):
            window = x_ref[v, :, at * cols : (at + PAIR + 4) * cols]
            scale = jnp.concatenate(
                [diff_ref[v, at + r : at + r + 1, :] for r in range(PAIR)], axis=1
            )
            spread = dot32(window, taps[...], NN) * (scale / 12.0)
            for p, part in enumerate(parts_of(spread, 2)):
                flux_ref[v, p, :, at * cols : (at + PAIR) * cols] = part

    def project(v):
        halo_wait(v)
        diffuse(v, 0, PAIR)
        diffuse(v, rows - PAIR, rows)
        wide, fine = parts[slot(v), 0], parts[slot(v), 1]
        accumulate(1, [(wide, flux_ref[v, 0]), (wide, flux_ref[v, 1]), (fine, flux_ref[v, 0])])

    def arrive(v):
        own_copy(v).wait()
        all_but_own(v, recv_sem).wait()
        relayout(v)

        @pl.when(me > 0)
        def _():
            to_low(v).start()

        @pl.when(me < n - 1)
        def _():
            to_high(v).start()

        @pl.when(me == 0)
        def _():
            x_ref[v, :, : 2 * cols] = jnp.zeros((total, 2 * cols), jnp.bfloat16)

        @pl.when(me == n - 1)
        def _():
            x_ref[v, :, (rows + 2) * cols :] = jnp.zeros((total, 2 * cols), jnp.bfloat16)

    tail = variables - 1

    @pl.loop(0, tail)
    def _(v):
        arrive(v)

        @pl.when(v + ahead < variables)
        def _():
            send_phase(v + ahead, ())

        @pl.when(v > 0)
        def _():
            project(v - 1)

        gram(v)
        diffuse(v, PAIR, rows - PAIR)

    core, chip, chips = lax.rem(me, 2), lax.div(me, 2), n // 2
    partner = me + 1 - 2 * core
    lanes = total // 2
    extents = (lanes, total)
    shares = tuple(max(extent // chips, SUBLANES) for extent in extents)
    owners = tuple(extent // share for extent, share in zip(extents, shares))
    given = (packed, part_sums.at[1])
    halves = (gram_half, cross_half)
    pieces = (gram_pieces, cross_pieces)
    sums = (gram_ref, sums_ref)

    def remote(source, target, which, stage, device):
        return pltpu.make_async_remote_copy(
            src_ref=source,
            dst_ref=target,
            send_sem=sum_send.at[which, stage],
            recv_sem=sum_recv.at[which, stage],
            device_id={"gx": device},
            device_id_type=MESH,
        )

    def ledger(count, which, stage):
        ref = sums_ref.at[pl.ds(0, count)]
        return remote(ref, ref, which, stage, partner)

    def peer(k):
        return lax.rem(chip + k, chips)

    def is_owner(which, index, body, other=None):
        if owners[which] == chips:
            body()
            return
        pl.when(index < owners[which])(body)
        if other is not None:
            pl.when(index >= owners[which])(other)

    def mine(which, base):
        share = shares[which]
        return pl.ds(pl.multiple_of(base + chip * share, SUBLANES), share)

    def pack():
        low, high = part_sums[0, 0, :lanes], part_sums[0, 1, lanes:]
        row, lane = iota((lanes, lanes), 0), iota((lanes, lanes), 1)
        packed[0, :lanes] = part_sums[0, 1, :lanes]
        packed[1, :lanes] = jnp.where(row >= lane, low, high)
        diagonal = jnp.sum(jnp.where(row == lane, high, 0.0), axis=0, keepdims=True)
        for h in range(2):
            packed[h, lanes:] = jnp.broadcast_to(diagonal, (SUBLANES, lanes))

    def pair_up(which):
        return remote(given[which].at[1 - core], halves[which], which, 0, partner)

    def scatter(which):
        pair_up(which).wait()
        half = halves[which]
        half[...] += given[which][core]
        share = shares[which]

        def send(k, carry):
            def start():
                piece = half.at[pl.ds(pl.multiple_of(peer(k) * share, SUBLANES), share)]
                remote(piece, pieces[which].at[k - 1], which, 1, 2 * peer(k) + core).start()

            is_owner(which, peer(k), start)
            if which == 0:
                remote(
                    half.at[pl.ds(lanes, SUBLANES)], diagonals.at[chip], 0, 3, 2 * peer(k) + core
                ).start()
            return carry

        lax.fori_loop(1, chips, send, 0, unroll=True)
        if which == 0:
            diagonals[chip] = half[lanes:]

    def spread_out(which):
        share, half = shares[which], halves[which]

        def owned():
            ledger((owners[which] - 1) * share, which, 1).wait_send()
            remote(pieces[which], pieces[which], which, 1, partner).wait_recv()
            acc = half[mine(which, 0), :]
            for k in range(chips - 1):
                acc += pieces[which][k]
            place = mine(which, core * extents[which])
            sums[which][place, :] = acc

            piece = sums[which].at[place]
            for k in range(1, n if which == 0 else chips):
                device = member(n - k) if which == 0 else 2 * peer(k) + core
                remote(piece, piece, which, 2, device).start()

        def others():
            ledger(owners[which] * share, which, 1).wait_send()

        is_owner(which, chip, owned, others)

    def hand_over():
        got = sums_ref.at[pl.ds(0, total - shares[1])]
        remote(got, got, 1, 2, partner).wait()
        done = sums_ref.at[pl.ds(core * total, total)]
        remote(done, done, 1, 3, partner).start()

    def finish(which):
        share = shares[which]
        full = 2 * extents[which]
        if which == 1:
            done = sums_ref.at[pl.ds(0, total)]
            remote(done, done, 1, 3, partner).wait()
            return

        def owned():
            got = sums[which].at[pl.ds(0, full - share)]
            remote(got, got, which, 2, partner).wait_recv()
            ledger((n - 1) * share, which, 2).wait_send()

        def others():
            remote(sums[which], sums[which], which, 2, partner).wait_recv()

        is_owner(which, chip, owned, others)

    def unpack():
        others = diagonals.at[pl.ds(0, chips - 1)]
        remote(others, others, 0, 3, partner).wait()
        scale = 1.0 / cells
        diagonal = diagonals[0]
        for k in range(1, chips):
            diagonal += diagonals[k]
        mixed = gram_ref[lanes:]
        turned = mixed.T
        row, lane = iota((lanes, lanes), 0), iota((lanes, lanes), 1)
        work[:lanes, :lanes] = jnp.where(row >= lane, mixed, turned) * scale
        work[:lanes, lanes:total] = gram_ref[:lanes] * scale
        high = jnp.where(row == lane, diagonal[:1], jnp.where(row < lane, mixed, turned))
        work[lanes:, lanes:total] = high * scale

    arrive(tail)
    gram(tail)
    pack()
    pair_up(0).start()
    scatter(0)
    if tail > 0:
        project(tail - 1)
    diffuse(tail, PAIR, rows - PAIR)
    spread_out(0)
    project(tail)
    pair_up(1).start()
    finish(0)
    unpack()
    scatter(1)
    for step in factor(work, rotation_ref):
        if step == 2:
            spread_out(1)
    rotation_parts = parts_of(rotation_ref[...], 2)

    @pl.loop(0, tail)
    def _(v):
        rotate(rotation_parts, flux_ref, v, turned, field_ref)

    hand_over()
    rotate(rotation_parts, flux_ref, tail, turned, field_ref)
    finish(1)

    for v in range(variables):
        all_but_own(v, send_sem).wait()


def dot_exact(a, b, dims):
    return lax.dot_general(a, b, dims, precision=HIGHEST, preferred_element_type=jnp.float32)


def eliminate(block, base):
    count, lanes = block.shape
    row = iota((count, lanes), 0)
    columns = [
        jnp.broadcast_to(block[:, k : k + 1], (count, lanes)) for k in range(base, base + PANEL)
    ]
    for k in range(0, PANEL, 2):
        one, two = columns[k], columns[k + 1]
        a, b, d = one[k : k + 1], one[k + 1 : k + 2], two[k + 1 : k + 2]
        det = a * d - b * b
        inverse_a, inverse_det = 1.0 / a, 1.0 / det
        below = row > k + 1
        of_one = jnp.where(
            below, (one * d - two * b) * inverse_det, jnp.where(row == k + 1, b * inverse_a, 0.0)
        )
        of_two = jnp.where(below, (two * a - one * b) * inverse_det, 0.0)
        for i in range(k + 2, PANEL):
            column = columns[i]
            columns[i] = column - of_one * column[k : k + 1] - of_two * column[k + 1 : k + 2]
        block = block - of_one * block[k : k + 1] - of_two * block[k + 1 : k + 2]
    return block


def factor(work, rotation_ref):
    size, lanes = rotation_ref.shape[0], 128
    row = iota((PIVOTS, lanes), 0)
    lane = iota((PIVOTS, lanes), 1)

    def cut(rows, first):
        group, shift = first // lanes * lanes, first % lanes
        block = work[rows : rows + PIVOTS, group : group + lanes]
        return pltpu.roll(block, lanes - shift, 1) if shift else block

    ahead = cut(0, 0)
    for first in range(0, size, PIVOTS):
        last = first + PIVOTS
        group = first // lanes * lanes
        stop = size + group + lanes
        block = jnp.where(lane < PIVOTS, ahead, jnp.where(lane == row + PIVOTS, 1.0, 0.0))
        done = []
        for base in range(0, PIVOTS, PANEL):
            block = eliminate(block, base)
            done.append(block[:PANEL])
            block = block[PANEL:]
        block = jnp.concatenate(done, axis=0)
        pivots = jnp.sum(jnp.where(lane == row, block, 0.0), axis=1, keepdims=True)
        inverse = pltpu.roll(block, lanes - PIVOTS, 1) / jnp.sqrt(pivots)
        inverse = inverse[:, :PIVOTS]
        if last < size:
            side = dot_exact(inverse, cut(first, last), NN)
            ahead = cut(last, last) - dot_exact(side[:, :PIVOTS], side, TN)
        stripe = dot_exact(inverse, work[first:last, group:stop], NN)
        rotation_ref[first:last, : group + lanes] = stripe[:, size - group :]
        if last < size:
            low = last // lanes * lanes
            work[low:, low:stop] -= dot_exact(
                stripe[:, low - group : size - group], stripe[:, low - group :], TN
            )
        yield first // PIVOTS


def gather(n, cells, snapshots, cell_weights, diffusivity):
    own, variables, _, cols = snapshots.shape
    rows = cell_weights.shape[0]
    total = own * n
    vmem = pl.BlockSpec(memory_space=pltpu.VMEM)
    chips, lanes = n // 2, total // 2
    dma = pltpu.SemaphoreType.DMA
    return pl.pallas_call(
        functools.partial(gather_kernel, n, float(cells)),
        out_shape=(
            pltpu.VMEM((variables, total, rows, cols), jnp.bfloat16),
            pltpu.VMEM((2 * total, total // 2), jnp.float32),
            pltpu.VMEM((total, total), jnp.float32),
        ),
        in_specs=[pl.BlockSpec(memory_space=pltpu.HBM)] * 3,
        out_specs=(vmem,) * 3,
        scratch_shapes=[
            pltpu.VMEM((rows, total, cols), jnp.bfloat16),
            pltpu.VMEM((variables, 2, total, rows * cols), jnp.bfloat16),
            pltpu.VMEM(cell_weights.shape, jnp.float32),
            pltpu.VMEM(diffusivity.shape, jnp.float32),
            pltpu.VMEM((total, variables, rows, cols), jnp.bfloat16),
            pltpu.VMEM((variables, total, (rows + 4) * cols), jnp.bfloat16),
            pltpu.VMEM((2, 3, total, rows * cols), jnp.bfloat16),
            pltpu.VMEM(((PAIR + 4) * cols, PAIR * cols), jnp.bfloat16),
            pltpu.VMEM((2, 2, total, total // 2), jnp.float32),
            pltpu.VMEM((2, lanes + SUBLANES, lanes), jnp.float32),
            pltpu.VMEM((lanes + SUBLANES, lanes), jnp.float32),
            pltpu.VMEM((total, lanes), jnp.float32),
            pltpu.VMEM((chips - 1, max(lanes // chips, SUBLANES), lanes), jnp.float32),
            pltpu.VMEM((chips - 1, max(total // chips, SUBLANES), lanes), jnp.float32),
            pltpu.VMEM((chips, SUBLANES, lanes), jnp.float32),
            pltpu.VMEM((total, lanes), jnp.float32),
            pltpu.VMEM((total, 2 * total), jnp.float32),
            dma((variables,)),
            dma((2,)),
            dma((variables,)),
            dma((variables,)),
            dma((2, variables)),
            dma((2, variables)),
            dma((2, 4)),
            dma((2, 4)),
        ],
        compiler_params=pltpu.CompilerParams(
            collective_id=0, has_side_effects=True, vmem_limit_bytes=GATHER_VMEM
        ),
        name="gather",
    )(snapshots, cell_weights, diffusivity)


def rotate(parts, flux_ref, v, turned, field_ref):
    rows, total, cols = turned.shape
    wide, fine = parts
    swap = swap_matrix(PACK, rows)
    for at in range(0, rows, PAIR):
        lanes = slice(at * cols, (at + PAIR) * cols)
        top, rest = flux_ref[v, 0, :, lanes], flux_ref[v, 1, :, lanes]
        acc = dot32(wide, top, NN) + dot32(wide, rest, NN) + dot32(fine, top, NN)
        for r in range(PAIR):
            turned[at + r] = acc[:, r * cols : (r + 1) * cols].astype(jnp.bfloat16)
    for g in range(0, total // PACK, 2):
        blocks = [
            turned[:, PACK * (g + h) : PACK * (g + h + 1), :].reshape(rows * PACK, cols)
            for h in range(2)
        ]
        done = dot32(swap, jnp.concatenate(blocks, axis=1), NN).astype(jnp.bfloat16)
        for h in range(2):
            field_ref[v, PACK * (g + h) : PACK * (g + h + 1)] = done[
                :, h * cols : (h + 1) * cols
            ].reshape(PACK, rows, cols)


def finish_kernel(cells, rotation_ref, sums_ref, field_ref, out_ref, reduced_ref, out_sem):
    variables, total = field_ref.shape[:2]

    def out_copy(v):
        return pltpu.make_async_copy(field_ref.at[v], out_ref.at[:, v], out_sem.at[v])

    for v in range(variables):
        out_copy(v).start()
    rotation = rotation_ref[...]
    cross = jnp.concatenate([sums_ref[:total], sums_ref[total:]], axis=1) * (1.0 / cells)
    product = dot_exact(rotation, cross, NN)
    reduced_ref[...] = dot_exact(product, rotation, NT)
    for v in range(variables):
        out_copy(v).wait()


def finish(cells, rotation, sums, fields):
    variables, total, rows, cols = fields.shape
    vmem = pl.BlockSpec(memory_space=pltpu.VMEM)
    return pl.pallas_call(
        functools.partial(finish_kernel, float(cells)),
        out_shape=(
            jax.ShapeDtypeStruct((total, variables, rows, cols), jnp.bfloat16),
            jax.ShapeDtypeStruct((total, total), jnp.float32),
        ),
        in_specs=[vmem] * 3,
        out_specs=(pl.BlockSpec(memory_space=pl.ANY), vmem),
        scratch_shapes=[pltpu.SemaphoreType.DMA((variables,))],
        compiler_params=pltpu.CompilerParams(vmem_limit_bytes=FINISH_VMEM),
        name="finish",
    )(rotation, sums, fields)


def on_device(n, snapshots, cell_weights, diffusivity):
    variables, rows, cols = diffusivity.shape
    cells = variables * rows * cols * n
    fields, sums, rotation = gather(n, cells, snapshots, cell_weights, diffusivity)
    return finish(cells, rotation, sums, fields)


def solution(mesh):
    in_specs = (
        P("gx", None, "groups", None),
        P(("groups", "gx"), None),
        P(None, ("groups", "gx"), None),
    )
    out_specs = (P(None, None, ("groups", "gx"), None), P("groups", None))
    return jax.shard_map(
        functools.partial(on_device, mesh.shape["gx"]),
        mesh=mesh, in_specs=in_specs, out_specs=out_specs, check_vma=False,
    )
```

```python
import functools

import jax
import jax.numpy as jnp
from jax import lax
from jax.experimental import pallas as pl
from jax.experimental.pallas import tpu as pltpu
from jax.sharding import PartitionSpec as P

MESH = pl.DeviceIdType.MESH
HIGHEST = lax.Precision.HIGHEST
NT = (((1,), (1,)), ((), ()))
TN = (((0,), (0,)), ((), ()))
NN = (((1,), (0,)), ((), ()))
PACK = 16
PIVOTS = 64
PANEL = 16
SUBLANES = 8
PAIR = 2
GATHER_VMEM = 54 * 2**20
FINISH_VMEM = 40 * 2**20


def iota(shape, dim):
    return lax.broadcasted_iota(jnp.int32, shape, dim)


def swap_matrix(outer, inner):
    size = outer * inner
    row, col = iota((size, size), 0), iota((size, size), 1)
    source = lax.rem(row, inner) * outer + lax.div(row, inner)
    return jnp.where(col == source, 1.0, 0.0).astype(jnp.bfloat16)


def parts_of(value, count):
    parts = []
    for _ in range(count):
        part = value.astype(jnp.bfloat16)
        parts.append(part)
        value = value - part.astype(jnp.float32)
    return parts


def dot32(a, b, dims):
    return lax.dot_general(a, b, dims, preferred_element_type=jnp.float32)


def stencil_tap(offset, gap):
    if offset == 0:
        along = jnp.where(gap == 0, -60.0, 0.0) + jnp.where(gap == 1, 16.0, 0.0)
        return along - jnp.where(gap == 2, 1.0, 0.0)
    weight = {1: 16.0, 2: -1.0}.get(abs(offset), 0.0)
    return jnp.where(gap == 0, weight, 0.0)


def gather_kernel(n, cells, snap_ref, weight_hbm, diff_hbm, field_ref, sums_ref, rotation_ref,
                  turned, flux_ref, weight_ref, diff_ref, pod, x_ref, parts, taps, part_sums, packed, gram_half,
                  cross_half, gram_pieces, cross_pieces, diagonals, gram_ref, work, local_sem,
                  grid_sem, send_sem, recv_sem, halo_send, halo_recv, sum_send, sum_recv,
                  edge_pod, edge_local, edge_send, edge_recv):
    me = lax.axis_index("gx")
    own, variables, _, cols = snap_ref.shape
    total, rows = pod.shape[0], pod.shape[2]

    barrier = pltpu.get_barrier_semaphore()

    def greet(k, carry):
        pl.semaphore_signal(
            barrier, inc=1, device_id={"gx": lax.rem(me + k, n)}, device_id_type=MESH
        )
        return carry

    lax.fori_loop(1, n, greet, 0)

    def own_copy(v):
        return pltpu.make_async_copy(
            snap_ref.at[:, v, pl.ds(me * rows, rows)],
            pod.at[pl.ds(me * own, own), v],
            local_sem.at[v],
        )

    def member(k):
        return me ^ k if n & (n - 1) == 0 else lax.rem(me + k, n)

    def send(v, k):
        target = member(k)
        pltpu.make_async_remote_copy(
            src_ref=snap_ref.at[:, v, pl.ds(target * rows, rows)],
            dst_ref=pod.at[pl.ds(me * own, own), v],
            send_sem=send_sem.at[v],
            recv_sem=recv_sem.at[v],
            device_id={"gx": target},
            device_id_type=MESH,
        ).start()

    side = lax.div(me, n // 2)
    edge_owner = n // 2 - 1 + side
    edge_source = n // 2 - side

    def edge_refs(v):
        place = pl.ds((me - side * (n // 2)) * own, own)
        return snap_ref.at[:, v, pl.ds(edge_source * rows, rows)], edge_pod.at[v, place]

    def own_edge(v):
        return pltpu.make_async_copy(*edge_refs(v), edge_local.at[v])

    def edge_copy(v):
        source, target = edge_refs(v)
        return pltpu.make_async_remote_copy(
            src_ref=source,
            dst_ref=target,
            send_sem=edge_send.at[v],
            recv_sem=edge_recv.at[v],
            device_id={"gx": edge_owner},
            device_id_type=MESH,
        )

    def send_edge(v):
        @pl.when(me == edge_owner)
        def _():
            own_edge(v).start()

        @pl.when(me != edge_owner)
        def _():
            edge_copy(v).start()

    def send_phase(v, near):
        for i in range(n - n // 2):
            send(v, n // 2 + i)
            if i + 1 < n // 2:
                for w in near:
                    send(w, i + 1)
                    if i == 0:
                        send_edge(w)

    grid_copies = [
        pltpu.make_async_copy(weight_hbm, weight_ref, grid_sem.at[0]),
        pltpu.make_async_copy(diff_hbm, diff_ref, grid_sem.at[1]),
    ]
    for copy in grid_copies:
        copy.start()
    for v in range(variables):
        own_copy(v).start()
    pl.semaphore_wait(barrier, n - 1)
    ahead = min(2, variables)
    each = -(-variables // ahead)
    for v in range(ahead):
        send_phase(v, range(v * each, min((v + 1) * each, variables)))

    part_sums[...] = jnp.zeros_like(part_sums)
    rotation_ref[...] = jnp.zeros_like(rotation_ref)
    work[:, total:] = jnp.where(iota((total, total), 0) == iota((total, total), 1), 1.0, 0.0)
    for copy in grid_copies:
        copy.wait()
    for k in range(PAIR + 4):
        for r in range(PAIR):
            gap = jnp.abs(iota((cols, cols), 0) - iota((cols, cols), 1))
            tap = stencil_tap(k - r - 2, gap)
            taps[k * cols : (k + 1) * cols, r * cols : (r + 1) * cols] = tap.astype(jnp.bfloat16)
    swap = swap_matrix(rows, PACK)

    def all_but_own(v, sem):
        piece = pod.at[pl.ds(0, total - own), v]
        return pltpu.make_async_copy(piece, piece, sem.at[v])

    middle, near_total = n // 2, total // 2

    def strip(v, at, part):
        first, count = ((0, total), (0, near_total), (near_total, near_total))[part]
        return x_ref.at[v, pl.ds(first, count), pl.ds(at * cols, 2 * cols)]

    def to_low(v, part=0):
        return pltpu.make_async_remote_copy(
            src_ref=strip(v, 2, part),
            dst_ref=strip(v, rows + 2, part),
            send_sem=halo_send.at[0, v],
            recv_sem=halo_recv.at[0, v],
            device_id={"gx": jnp.maximum(me - 1, 0)},
            device_id_type=MESH,
        )

    def to_high(v, part=0):
        return pltpu.make_async_remote_copy(
            src_ref=strip(v, rows, part),
            dst_ref=strip(v, 0, part),
            send_sem=halo_send.at[1, v],
            recv_sem=halo_recv.at[1, v],
            device_id={"gx": jnp.minimum(me + 1, n - 1)},
            device_id_type=MESH,
        )

    def beyond(v):
        own_edge(v).wait()
        piece = edge_pod.at[v, pl.ds(0, near_total - own)]
        pltpu.make_async_copy(piece, piece, edge_recv.at[v]).wait()

    def turn_edge(v, first_snapshot, first_row, lanes_at):
        for g in range(0, near_total // PACK, 2):
            blocks = [
                edge_pod[v, PACK * (g + h) : PACK * (g + h + 1)].reshape(PACK * rows, cols)
                for h in range(2)
            ]
            turned_edge = dot32(swap, jnp.concatenate(blocks, axis=1), NN).astype(jnp.bfloat16)
            for h in range(2):
                at = first_snapshot + PACK * (g + h)
                for r in range(2):
                    place = (lanes_at + r) * cols
                    x_ref[v, at : at + PACK, place : place + cols] = turned_edge[
                        (first_row + r) * PACK : (first_row + r + 1) * PACK,
                        h * cols : (h + 1) * cols,
                    ]

    def relayout(v):
        for g in range(0, total // PACK, 2):
            blocks = [
                pod[PACK * (g + h) : PACK * (g + h + 1), v].reshape(PACK * rows, cols)
                for h in range(2)
            ]
            turned = dot32(swap, jnp.concatenate(blocks, axis=1), NN).astype(jnp.bfloat16)
            for h in range(2):
                for at in range(rows):
                    x_ref[v, PACK * (g + h) : PACK * (g + h + 1), (at + 2) * cols : (at + 3) * cols] = (
                        turned[at * PACK : (at + 1) * PACK, h * cols : (h + 1) * cols]
                    )

    def accumulate(which, pairs):
        acc = dot32(*pairs[0], NT)
        for left, right in pairs[1:]:
            acc += dot32(left, right, NT)
        part_sums[which, 0] += acc[:, : total // 2]
        part_sums[which, 1] += acc[:, total // 2 :]

    def slot(v):
        return lax.rem(v, 2)

    def gram(v):
        for at in range(rows):
            field = x_ref[v, :, (at + 2) * cols : (at + 3) * cols].astype(jnp.float32)
            for p, part in enumerate(parts_of(field * weight_ref[at : at + 1, :], 3)):
                parts[slot(v), p, :, at * cols : (at + 1) * cols] = part
        left = x_ref[v, :, 2 * cols : (rows + 2) * cols]
        accumulate(0, [(left, parts[slot(v), p]) for p in range(3)])

    def halo_wait(v):
        @pl.when((me < n - 1) & (me != middle - 1))
        def _():
            to_low(v).wait_recv()
            to_high(v).wait_send()

        @pl.when((me > 0) & (me != middle))
        def _():
            to_high(v).wait_recv()
            to_low(v).wait_send()

        @pl.when(me == middle - 1)
        def _():
            to_low(v, 2).wait_recv()
            to_high(v, 1).wait_send()

        @pl.when(me == middle)
        def _():
            to_high(v, 1).wait_recv()
            to_low(v, 2).wait_send()

    def diffuse(v, first, last):
        for at in range(first, last, PAIR):
            window = x_ref[v, :, at * cols : (at + PAIR + 4) * cols]
            scale = jnp.concatenate(
                [diff_ref[v, at + r : at + r + 1, :] for r in range(PAIR)], axis=1
            )
            spread = dot32(window, taps[...], NN) * (scale / 12.0)
            for p, part in enumerate(parts_of(spread, 2)):
                flux_ref[v, p, :, at * cols : (at + PAIR) * cols] = part

    def project(v):
        halo_wait(v)
        diffuse(v, 0, PAIR)
        diffuse(v, rows - PAIR, rows)
        wide, fine = parts[slot(v), 0], parts[slot(v), 1]
        accumulate(1, [(wide, flux_ref[v, 0]), (wide, flux_ref[v, 1]), (fine, flux_ref[v, 0])])

    def arrive(v):
        own_copy(v).wait()
        all_but_own(v, recv_sem).wait()
        relayout(v)

    def share_edges(v):
        @pl.when((me > 0) & (me != middle))
        def _():
            to_low(v).start()

        @pl.when((me < n - 1) & (me != middle - 1))
        def _():
            to_high(v).start()

        @pl.when(me == middle)
        def _():
            to_low(v, 2).start()
            beyond(v)
            turn_edge(v, near_total, rows - 2, 0)

        @pl.when(me == middle - 1)
        def _():
            to_high(v, 1).start()
            beyond(v)
            turn_edge(v, 0, 0, rows + 2)

        @pl.when(me == 0)
        def _():
            x_ref[v, :, : 2 * cols] = jnp.zeros((total, 2 * cols), jnp.bfloat16)

        @pl.when(me == n - 1)
        def _():
            x_ref[v, :, (rows + 2) * cols :] = jnp.zeros((total, 2 * cols), jnp.bfloat16)

    tail = variables - 1

    @pl.loop(0, tail)
    def _(v):
        arrive(v)
        share_edges(v)

        @pl.when(v + ahead < variables)
        def _():
            send_phase(v + ahead, ())

        @pl.when(v > 0)
        def _():
            project(v - 1)

        gram(v)
        diffuse(v, PAIR, rows - PAIR)

    core, chip, chips = lax.rem(me, 2), lax.div(me, 2), n // 2
    partner = me + 1 - 2 * core
    lanes = total // 2
    extents = (lanes, total)
    shares = tuple(max(extent // chips, SUBLANES) for extent in extents)
    owners = tuple(extent // share for extent, share in zip(extents, shares))
    given = (packed, part_sums.at[1])
    halves = (gram_half, cross_half)
    pieces = (gram_pieces, cross_pieces)
    sums = (gram_ref, sums_ref)

    def remote(source, target, which, stage, device):
        return pltpu.make_async_remote_copy(
            src_ref=source,
            dst_ref=target,
            send_sem=sum_send.at[which, stage],
            recv_sem=sum_recv.at[which, stage],
            device_id={"gx": device},
            device_id_type=MESH,
        )

    def ledger(count, which, stage):
        ref = sums_ref.at[pl.ds(0, count)]
        return remote(ref, ref, which, stage, partner)

    def peer(k):
        return lax.rem(chip + k, chips)

    def is_owner(which, index, body, other=None):
        if owners[which] == chips:
            body()
            return
        pl.when(index < owners[which])(body)
        if other is not None:
            pl.when(index >= owners[which])(other)

    def mine(which, base):
        share = shares[which]
        return pl.ds(pl.multiple_of(base + chip * share, SUBLANES), share)

    def pack():
        low, high = part_sums[0, 0, :lanes], part_sums[0, 1, lanes:]
        row, lane = iota((lanes, lanes), 0), iota((lanes, lanes), 1)
        packed[0, :lanes] = part_sums[0, 1, :lanes]
        packed[1, :lanes] = jnp.where(row >= lane, low, high)
        diagonal = jnp.sum(jnp.where(row == lane, high, 0.0), axis=0, keepdims=True)
        for h in range(2):
            packed[h, lanes:] = jnp.broadcast_to(diagonal, (SUBLANES, lanes))

    def pair_up(which):
        return remote(given[which].at[1 - core], halves[which], which, 0, partner)

    def scatter(which):
        pair_up(which).wait()
        half = halves[which]
        half[...] += given[which][core]
        share = shares[which]

        def send(k, carry):
            def start():
                piece = half.at[pl.ds(pl.multiple_of(peer(k) * share, SUBLANES), share)]
                remote(piece, pieces[which].at[k - 1], which, 1, 2 * peer(k) + core).start()

            is_owner(which, peer(k), start)
            if which == 0:
                remote(
                    half.at[pl.ds(lanes, SUBLANES)], diagonals.at[chip], 0, 3, 2 * peer(k) + core
                ).start()
            return carry

        lax.fori_loop(1, chips, send, 0, unroll=True)
        if which == 0:
            diagonals[chip] = half[lanes:]

    def spread_out(which):
        share, half = shares[which], halves[which]

        def owned():
            ledger((owners[which] - 1) * share, which, 1).wait_send()
            remote(pieces[which], pieces[which], which, 1, partner).wait_recv()
            acc = half[mine(which, 0), :]
            for k in range(chips - 1):
                acc += pieces[which][k]
            place = mine(which, core * extents[which])
            sums[which][place, :] = acc

            piece = sums[which].at[place]
            for k in range(1, n if which == 0 else chips):
                device = member(n - k) if which == 0 else 2 * peer(k) + core
                remote(piece, piece, which, 2, device).start()

        def others():
            ledger(owners[which] * share, which, 1).wait_send()

        is_owner(which, chip, owned, others)

    def hand_over():
        got = sums_ref.at[pl.ds(0, total - shares[1])]
        remote(got, got, 1, 2, partner).wait()
        done = sums_ref.at[pl.ds(core * total, total)]
        remote(done, done, 1, 3, partner).start()

    def finish(which):
        share = shares[which]
        full = 2 * extents[which]
        if which == 1:
            done = sums_ref.at[pl.ds(0, total)]
            remote(done, done, 1, 3, partner).wait()
            return

        def owned():
            got = sums[which].at[pl.ds(0, full - share)]
            remote(got, got, which, 2, partner).wait_recv()
            ledger((n - 1) * share, which, 2).wait_send()

        def others():
            remote(sums[which], sums[which], which, 2, partner).wait_recv()

        is_owner(which, chip, owned, others)

    def unpack():
        others = diagonals.at[pl.ds(0, chips - 1)]
        remote(others, others, 0, 3, partner).wait()
        scale = 1.0 / cells
        diagonal = diagonals[0]
        for k in range(1, chips):
            diagonal += diagonals[k]
        mixed = gram_ref[lanes:]
        turned = mixed.T
        row, lane = iota((lanes, lanes), 0), iota((lanes, lanes), 1)
        work[:lanes, :lanes] = jnp.where(row >= lane, mixed, turned) * scale
        work[:lanes, lanes:total] = gram_ref[:lanes] * scale
        high = jnp.where(row == lane, diagonal[:1], jnp.where(row < lane, mixed, turned))
        work[lanes:, lanes:total] = high * scale

    arrive(tail)
    gram(tail)
    pack()
    pair_up(0).start()
    scatter(0)
    share_edges(tail)
    if tail > 0:
        project(tail - 1)
    diffuse(tail, PAIR, rows - PAIR)
    spread_out(0)
    project(tail)
    pair_up(1).start()
    finish(0)
    unpack()
    scatter(1)
    for step in factor(work, rotation_ref):
        if step == 2:
            spread_out(1)
    rotation_parts = parts_of(rotation_ref[...], 2)

    @pl.loop(0, tail)
    def _(v):
        rotate(rotation_parts, flux_ref, v, turned, field_ref)

    hand_over()
    rotate(rotation_parts, flux_ref, tail, turned, field_ref)
    finish(1)

    for v in range(variables):
        all_but_own(v, send_sem).wait()

        @pl.when(me != edge_owner)
        def _():
            edge_copy(v).wait_send()


def dot_exact(a, b, dims):
    return lax.dot_general(a, b, dims, precision=HIGHEST, preferred_element_type=jnp.float32)


def eliminate(block, base):
    count, lanes = block.shape
    row = iota((count, lanes), 0)
    columns = [
        jnp.broadcast_to(block[:, k : k + 1], (count, lanes)) for k in range(base, base + PANEL)
    ]
    for k in range(0, PANEL, 2):
        one, two = columns[k], columns[k + 1]
        a, b, d = one[k : k + 1], one[k + 1 : k + 2], two[k + 1 : k + 2]
        det = a * d - b * b
        inverse_a, inverse_det = 1.0 / a, 1.0 / det
        below = row > k + 1
        of_one = jnp.where(
            below, (one * d - two * b) * inverse_det, jnp.where(row == k + 1, b * inverse_a, 0.0)
        )
        of_two = jnp.where(below, (two * a - one * b) * inverse_det, 0.0)
        for i in range(k + 2, PANEL):
            column = columns[i]
            columns[i] = column - of_one * column[k : k + 1] - of_two * column[k + 1 : k + 2]
        block = block - of_one * block[k : k + 1] - of_two * block[k + 1 : k + 2]
    return block


def factor(work, rotation_ref):
    size, lanes = rotation_ref.shape[0], 128
    row = iota((PIVOTS, lanes), 0)
    lane = iota((PIVOTS, lanes), 1)

    def cut(rows, first):
        group, shift = first // lanes * lanes, first % lanes
        block = work[rows : rows + PIVOTS, group : group + lanes]
        return pltpu.roll(block, lanes - shift, 1) if shift else block

    ahead = cut(0, 0)
    for first in range(0, size, PIVOTS):
        last = first + PIVOTS
        group = first // lanes * lanes
        stop = size + group + lanes
        block = jnp.where(lane < PIVOTS, ahead, jnp.where(lane == row + PIVOTS, 1.0, 0.0))
        done = []
        for base in range(0, PIVOTS, PANEL):
            block = eliminate(block, base)
            done.append(block[:PANEL])
            block = block[PANEL:]
        block = jnp.concatenate(done, axis=0)
        pivots = jnp.sum(jnp.where(lane == row, block, 0.0), axis=1, keepdims=True)
        inverse = pltpu.roll(block, lanes - PIVOTS, 1) / jnp.sqrt(pivots)
        inverse = inverse[:, :PIVOTS]
        if last < size:
            side = dot_exact(inverse, cut(first, last), NN)
            ahead = cut(last, last) - dot_exact(side[:, :PIVOTS], side, TN)
        stripe = dot_exact(inverse, work[first:last, group:stop], NN)
        rotation_ref[first:last, : group + lanes] = stripe[:, size - group :]
        if last < size:
            low = last // lanes * lanes
            work[low:, low:stop] -= dot_exact(
                stripe[:, low - group : size - group], stripe[:, low - group :], TN
            )
        yield first // PIVOTS


def gather(n, cells, snapshots, cell_weights, diffusivity):
    own, variables, _, cols = snapshots.shape
    rows = cell_weights.shape[0]
    total = own * n
    vmem = pl.BlockSpec(memory_space=pltpu.VMEM)
    chips, lanes = n // 2, total // 2
    dma = pltpu.SemaphoreType.DMA
    return pl.pallas_call(
        functools.partial(gather_kernel, n, float(cells)),
        out_shape=(
            pltpu.VMEM((variables, total, rows, cols), jnp.bfloat16),
            pltpu.VMEM((2 * total, total // 2), jnp.float32),
            pltpu.VMEM((total, total), jnp.float32),
        ),
        in_specs=[pl.BlockSpec(memory_space=pltpu.HBM)] * 3,
        out_specs=(vmem,) * 3,
        scratch_shapes=[
            pltpu.VMEM((total * rows, cols), jnp.float32),
            pltpu.VMEM((variables, 2, total, rows * cols), jnp.bfloat16),
            pltpu.VMEM(cell_weights.shape, jnp.float32),
            pltpu.VMEM(diffusivity.shape, jnp.float32),
            pltpu.VMEM((total, variables, rows, cols), jnp.bfloat16),
            pltpu.VMEM((variables, total, (rows + 4) * cols), jnp.bfloat16),
            pltpu.VMEM((2, 3, total, rows * cols), jnp.bfloat16),
            pltpu.VMEM(((PAIR + 4) * cols, PAIR * cols), jnp.bfloat16),
            pltpu.VMEM((2, 2, total, total // 2), jnp.float32),
            pltpu.VMEM((2, lanes + SUBLANES, lanes), jnp.float32),
            pltpu.VMEM((lanes + SUBLANES, lanes), jnp.float32),
            pltpu.VMEM((total, lanes), jnp.float32),
            pltpu.VMEM((chips - 1, max(lanes // chips, SUBLANES), lanes), jnp.float32),
            pltpu.VMEM((chips - 1, max(total // chips, SUBLANES), lanes), jnp.float32),
            pltpu.VMEM((chips, SUBLANES, lanes), jnp.float32),
            pltpu.VMEM((total, lanes), jnp.float32),
            pltpu.VMEM((total, 2 * total), jnp.float32),
            dma((variables,)),
            dma((2,)),
            dma((variables,)),
            dma((variables,)),
            dma((2, variables)),
            dma((2, variables)),
            dma((2, 4)),
            dma((2, 4)),
            pltpu.VMEM((variables, lanes, rows, cols), jnp.bfloat16),
            dma((variables,)),
            dma((variables,)),
            dma((variables,)),
        ],
        compiler_params=pltpu.CompilerParams(
            collective_id=0, has_side_effects=True, vmem_limit_bytes=GATHER_VMEM
        ),
        name="gather",
    )(snapshots, cell_weights, diffusivity)


def rotate(parts, flux_ref, v, turned, field_ref):
    total, rows, cols = field_ref.shape[1:]
    low = total // 2
    wide, fine = parts
    doubled = jnp.concatenate([wide[:low, :low]] * 2, axis=1)
    for at in range(0, rows, PAIR):
        lanes = slice(at * cols, (at + PAIR) * cols)
        top, rest = flux_ref[v, 0, :, lanes], flux_ref[v, 1, :, lanes]
        folded = jnp.concatenate([top[:low], rest[:low]], axis=0)
        upper = dot32(doubled, folded, NN) + dot32(fine[:low, :low], top[:low], NN)
        lower = dot32(wide[low:], top, NN) + dot32(wide[low:], rest, NN)
        lower += dot32(fine[low:], top, NN)
        acc = jnp.concatenate([upper, lower], axis=0)
        for r in range(PAIR):
            turned[pl.ds(at + r, total, stride=rows), :] = acc[:, r * cols : (r + 1) * cols]
    for first in range(0, total, 4 * PACK):
        block = turned[first * rows : (first + 4 * PACK) * rows, :].astype(jnp.bfloat16)
        field_ref[v, first : first + 4 * PACK] = block.reshape(4 * PACK, rows, cols)


def finish_kernel(cells, rotation_ref, sums_ref, field_ref, out_ref, reduced_ref, out_sem):
    variables, total = field_ref.shape[:2]

    def out_copy(v):
        return pltpu.make_async_copy(field_ref.at[v], out_ref.at[:, v], out_sem.at[v])

    for v in range(variables):
        out_copy(v).start()
    rotation = rotation_ref[...]
    cross = jnp.concatenate([sums_ref[:total], sums_ref[total:]], axis=1) * (1.0 / cells)
    product = dot_exact(rotation, cross, NN)
    reduced_ref[...] = dot_exact(product, rotation, NT)
    for v in range(variables):
        out_copy(v).wait()


def finish(cells, rotation, sums, fields):
    variables, total, rows, cols = fields.shape
    vmem = pl.BlockSpec(memory_space=pltpu.VMEM)
    return pl.pallas_call(
        functools.partial(finish_kernel, float(cells)),
        out_shape=(
            jax.ShapeDtypeStruct((total, variables, rows, cols), jnp.bfloat16),
            jax.ShapeDtypeStruct((total, total), jnp.float32),
        ),
        in_specs=[vmem] * 3,
        out_specs=(pl.BlockSpec(memory_space=pl.ANY), vmem),
        scratch_shapes=[pltpu.SemaphoreType.DMA((variables,))],
        compiler_params=pltpu.CompilerParams(vmem_limit_bytes=FINISH_VMEM),
        name="finish",
    )(rotation, sums, fields)


def on_device(n, snapshots, cell_weights, diffusivity):
    variables, rows, cols = diffusivity.shape
    cells = variables * rows * cols * n
    fields, sums, rotation = gather(n, cells, snapshots, cell_weights, diffusivity)
    return finish(cells, rotation, sums, fields)


def solution(mesh):
    in_specs = (
        P("gx", None, "groups", None),
        P(("groups", "gx"), None),
        P(None, ("groups", "gx"), None),
    )
    out_specs = (P(None, None, ("groups", "gx"), None), P("groups", None))
    return jax.shard_map(
        functools.partial(on_device, mesh.shape["gx"]),
        mesh=mesh, in_specs=in_specs, out_specs=out_specs, check_vma=False,
    )
```
